32 devices in a mesh: groups: 2 (over y), blk: 4 (over z), heads: 2 (over x), rows: 2 (over core).
Axes of the slice: x: 2, y: 2, z: 4, core: 2. Of those that a mesh axis runs over, the one named last changes fastest.
Arguments:
- queries: bfloat16 [64, 16, 256], P(('groups', 'blk', 'rows'), 'heads'), parts along dimension 0, may hold values from -128 to 128
- src_keys: bfloat16 [12288, 8, 256], P(('groups', 'blk'), 'heads'), parts along dimension 0, may hold values from -6 to 6
- src_values: bfloat16 [12288, 8, 256], P(('groups', 'blk'), 'heads'), parts along dimension 0, may hold values from -6 to 6
- dec_state: bfloat16 [64, 3584], P('groups', ('blk', 'rows')), parts along dimension 0, may hold values from -0.59765625 to 0.59765625
- mask_embed: bfloat16 [3584], P(('blk', 'rows')), may hold values from -1.796875 to 1.796875
- out_weight: bfloat16 [4096, 3584], P('heads', ('blk', 'rows')), may hold values from -0.09375 to 0.09375
- norm_gain: bfloat16 [3584], P(('blk', 'rows')), may hold values from 0.5 to 1.5
- gate_weight: bfloat16 [3584, 14336], P('heads', ('blk', 'rows')), may hold values from -0.09375 to 0.09375
- up_weight: bfloat16 [3584, 14336], P('heads', ('blk', 'rows')), may hold values from -0.09375 to 0.09375
- down_weight: bfloat16 [14336, 3584], P(('blk', 'rows'), 'heads'), may hold values from -0.046875 to 0.046875
- cand_lengths: int32 [2], P('groups'), parts along dimension 0, may hold values from 64 to 128
- masked_pos: int32 [2, 48], P('groups'), parts along dimension 0, may hold values from 0 to 127, as said below
Outputs:
- stream: bfloat16 [64, 3584], P('groups', ('blk', 'rows')), parts along dimension 0
- branch: bfloat16 [64, 3584], P(('groups', 'blk', 'rows'), 'heads'), parts along dimension 0
The draws below stay inside these ranges and needn't reach their ends.
There are 2 independent parts, one for each index of `groups`. The reference program is written for one: setup_inputs(seed, part) draws one part's arguments, and reference() takes and returns one part's arrays. A program takes and returns all parts, laid end to end along the dimension named above; an argument that names none is the same for every part. Nothing has to cross between parts.
Inputs may be any that keep to these rules, and one draw needn't show every extreme that they name: `masked_pos`: the 48 positions of one candidate are distinct.
All inputs are finite; a program needn't handle non-finite values.
Results may differ from the reference program's by a relative error of at most 0.03.
Values may be sent and summed in bfloat16 or wider, within the bound.
A program may use at most 64 MiB of HBM per device.

```python
import math
import jax
import jax.numpy as jnp
from jax import lax

D = 3584
FF = 14336
QH = 16
KVH = 8
HD = 256
LEN = 128
NMASK = 48
S_DEV = 1536
TOKENS = 32
CAND = 1
SRC = 6144


def source_and_queries(key):
    base_key = jax.random.fold_in(key, 11)
    key_one, key_two = jax.random.split(base_key, 2)
    keys_drawn = jnp.clip(jax.random.normal(key_one, (SRC, KVH, HD), jnp.float32), -6.0, 6.0)
    query_drawn = 2.5 * jnp.clip(jax.random.normal(key_two, (TOKENS, QH, HD), jnp.float32), -6.0, 6.0)
    return (keys_drawn, query_drawn)


def draw_src_keys(key, part):
    return source_and_queries(key)[0].astype(jnp.bfloat16)


def draw_queries(key, part):
    return source_and_queries(key)[1].astype(jnp.bfloat16)


def draw_masked_pos(key, part):
    scores = jax.random.randint(jax.random.fold_in(key, 5), (CAND, LEN), 0, 1 << 20) * LEN
    scores = scores + jnp.arange(LEN, dtype=jnp.int32)[None, :]
    order = jnp.argsort(scores, axis=1)
    return order[:, :NMASK].astype(jnp.int32)


def shard_levels(rng, dims, pieces, smallest, high):
    def one(axis_at, blocks):
        steps = jax.random.uniform(jax.random.fold_in(jax.random.fold_in(rng, 6), axis_at), (blocks,), jnp.float32, smallest / len(pieces), high / len(pieces))
        return jnp.repeat(jnp.exp(steps), dims[axis_at] // blocks).reshape((-1,) + (1,) * (len(dims) - axis_at - 1))

    gain = one(*pieces[0])
    for cut in pieces[1:]:
        gain = gain * one(*cut)
    return gain


def gaussian(rng, extent, deviation, limit, cuts=(), kind=jnp.bfloat16):
    drawn = jax.random.normal(rng, extent, jnp.float32) * deviation
    if len(cuts) > 0:
        drawn = shard_levels(rng, extent, cuts, -0.22, 0.18) * drawn
    return jnp.clip(drawn, min=-limit, max=limit).astype(kind)


def setup_inputs(seed: int = 0, part: int = 0) -> dict:
    arg_keys = jax.random.split(jax.random.key(seed), 13)
    part_splits = jax.random.split(jax.random.fold_in(arg_keys[12], part), 13)
    queries = draw_queries(jax.random.fold_in(jax.random.fold_in(arg_keys[12], part), 71), part)
    src_keys = draw_src_keys(jax.random.fold_in(jax.random.fold_in(arg_keys[12], part), 71), part)
    src_values = gaussian(part_splits[2], (SRC, KVH, HD), 1.0, 6.0, ((0, 4), (1, 2)))
    dec_state = gaussian(part_splits[3], (TOKENS, D), 0.1, 0.59765625, ((1, 8),))
    mask_embed = gaussian(arg_keys[4], (D,), 0.3, 1.796875, ((0, 8),))
    out_weight = gaussian(arg_keys[5], (QH * HD, D), (QH * HD) ** -0.5, 0.09375, ((0, 2), (1, 8)))
    norm_gain = jnp.clip(1.0 + 0.1 * jax.random.normal(arg_keys[6], (D,), jnp.float32), 0.5, 1.5).astype(jnp.bfloat16)
    gate_weight = gaussian(arg_keys[7], (D, FF), D ** -0.5, 0.09375, ((0, 2), (1, 8)))
    up_weight = gaussian(arg_keys[8], (D, FF), D ** -0.5, 0.09375, ((0, 2), (1, 8)))
    down_weight = gaussian(arg_keys[9], (FF, D), FF ** -0.5, 0.046875, ((0, 8), (1, 2)))
    cand_lengths = jax.random.randint(part_splits[10], (CAND,), LEN // 2, LEN + 1).astype(jnp.int32)
    masked_pos = draw_masked_pos(jax.random.fold_in(jax.random.fold_in(arg_keys[12], part), 71), part)
    return {"queries": queries, "src_keys": src_keys, "src_values": src_values, "dec_state": dec_state, "mask_embed": mask_embed, "out_weight": out_weight, "norm_gain": norm_gain, "gate_weight": gate_weight, "up_weight": up_weight, "down_weight": down_weight, "cand_lengths": cand_lengths, "masked_pos": masked_pos}


def token_masks(cand_lengths, masked_pos, tokens):
    positions = jnp.arange(tokens, dtype=jnp.int32) % LEN
    length_tok = jnp.repeat(cand_lengths, LEN)[:tokens]
    valid_tok = positions < length_tok
    slots = jnp.arange(LEN, dtype=jnp.int32)
    masked_tok = jnp.any(masked_pos[:, :, None] == slots[None, None, :], axis=1).reshape(-1)[:tokens]
    return (valid_tok, masked_tok)

def reference(queries, src_keys, src_values, dec_state, mask_embed, out_weight, norm_gain, gate_weight, up_weight, down_weight, cand_lengths, masked_pos):
    tokens = queries.shape[0]
    group_size = QH // KVH
    row_block = math.gcd(tokens, 32)
    src_blocks = SRC // S_DEV
    keys_wide = src_keys.astype(jnp.float32)
    values_wide = src_values.astype(jnp.float32).reshape(src_blocks, S_DEV, KVH, HD)
    score_scale = HD ** (-0.5)

    def attend(query_rows):
        grouped = query_rows.astype(jnp.float32).reshape(row_block, KVH, group_size, HD)
        scores = jnp.einsum('tgjd,kgd->tgjk', grouped, keys_wide, precision=lax.Precision.HIGHEST) * score_scale
        scores = scores.reshape(row_block, KVH, group_size, src_blocks, S_DEV)
        block_peak = lax.optimization_barrier(jnp.max(scores, axis=4))
        weights = jnp.exp(scores - block_peak[..., None])
        block_totals = lax.optimization_barrier(jnp.sum(weights, axis=4))
        rounded = weights.astype(jnp.bfloat16).astype(jnp.float32)
        block_numer = jnp.einsum('tgjbk,bkgd->tgjbd', rounded, values_wide, precision=lax.Precision.HIGHEST)
        top = lax.optimization_barrier(jnp.max(block_peak, axis=3, keepdims=True))
        factor = jnp.exp(block_peak - top)
        numerator = lax.optimization_barrier(jnp.sum(block_numer * factor[..., None], axis=3))
        totals = lax.optimization_barrier(jnp.sum(block_totals * factor, axis=3))
        return (numerator / totals[..., None]).astype(jnp.bfloat16).reshape(row_block, QH * HD)
    blocks = queries.reshape(tokens // row_block, row_block, QH, HD)
    attn_out = lax.map(attend, blocks).reshape(tokens, QH * HD)
    projected = jnp.dot(attn_out, out_weight, preferred_element_type=jnp.float32)
    valid_tok, masked_tok = token_masks(cand_lengths, masked_pos, tokens)
    base_state = jnp.where(masked_tok[:, None], mask_embed[None, :], dec_state).astype(jnp.float32)
    stream_mid = base_state + projected
    inv_rms = lax.rsqrt(lax.optimization_barrier(jnp.mean(stream_mid * stream_mid, axis=1, keepdims=True)) + 1e-06)
    normed = (stream_mid * inv_rms * norm_gain.astype(jnp.float32)).astype(jnp.bfloat16)
    gate_rows = jnp.dot(normed, gate_weight, preferred_element_type=jnp.float32)
    up_rows = jnp.dot(normed, up_weight, preferred_element_type=jnp.float32)
    hidden = (jax.nn.gelu(gate_rows, approximate=True) * up_rows).astype(jnp.bfloat16)
    down_out = jnp.dot(hidden, down_weight, preferred_element_type=jnp.float32)
    keep_mask = valid_tok.astype(jnp.float32)[:, None]
    return ((stream_mid * keep_mask).astype(jnp.bfloat16), (down_out * keep_mask).astype(jnp.bfloat16))
```

```python
import functools

import jax
import jax.numpy as jnp
from jax import lax
from jax.experimental import pallas as pl
from jax.experimental.pallas import tpu as pltpu
from jax.sharding import PartitionSpec as P

D = 3584
LEN = 128


def token_masks(cand_lengths, masked_pos, tokens):
    positions = jnp.arange(tokens, dtype=jnp.int32) % LEN
    length_tok = jnp.repeat(cand_lengths, LEN)[:tokens]
    valid_tok = positions < length_tok
    slots = jnp.arange(LEN, dtype=jnp.int32)
    masked_tok = jnp.any(masked_pos[:, :, None] == slots[None, None, :], axis=1).reshape(-1)[
        :tokens
    ]
    return (valid_tok, masked_tok)


def shards(
    queries,
    src_keys,
    src_values,
    dec_state,
    mask_embed,
    out_weight,
    norm_gain,
    gate_weight,
    up_weight,
    down_weight,
    cand_lengths,
    masked_pos,
):
    tok_dev, local_heads, head_size = queries.shape
    kv_local = src_keys.shape[1]
    group_size = local_heads // kv_local
    score_scale = head_size ** (-0.5)
    queries_all = lax.all_gather(queries, "blk", axis=0, tiled=True)
    gathered_rows = queries_all.shape[0]
    grouped = queries_all.reshape(gathered_rows, kv_local, group_size, head_size)
    scores = (
        jnp.einsum("tgjd,kgd->tgjk", grouped, src_keys, preferred_element_type=jnp.float32)
        * score_scale
    )
    local_peak = jnp.max(scores, axis=3)
    weights = jnp.exp(scores - local_peak[..., None])
    totals = jnp.sum(weights, axis=3)
    numerator = jnp.einsum(
        "tgjk,kgd->tgjd",
        weights.astype(jnp.bfloat16),
        src_values,
        preferred_element_type=jnp.float32,
    )
    highest = lax.pmax(local_peak, "blk")
    factor = jnp.exp(local_peak - highest)
    numer_own, totals_own = (
        lax.psum_scatter(
            (numerator * factor[..., None]).astype(jnp.bfloat16),
            "blk",
            scatter_dimension=0,
            tiled=True,
        ).astype(jnp.float32),
        lax.psum_scatter(
            (totals * factor).astype(jnp.bfloat16), "blk", scatter_dimension=0, tiled=True
        ).astype(jnp.float32),
    )
    attn_own = (
        (numer_own / totals_own[..., None])
        .astype(jnp.bfloat16)
        .reshape(tok_dev, local_heads * head_size)
    )
    attn_all = lax.all_gather(attn_own, ("blk", "rows"), axis=0, tiled=True)
    tokens = attn_all.shape[0]
    projected = lax.psum(
        jnp.dot(attn_all, out_weight, preferred_element_type=jnp.float32).astype(jnp.bfloat16),
        "heads",
    ).astype(jnp.float32)
    valid_tok, masked_tok = token_masks(cand_lengths, masked_pos, tokens)
    base_state = jnp.where(masked_tok[:, None], mask_embed[None, :], dec_state).astype(jnp.float32)
    stream_mid = base_state + projected
    squares = lax.psum(jnp.sum(stream_mid * stream_mid, axis=1), ("blk", "rows"))
    inv_rms = lax.rsqrt(squares / D + 1e-06)[:, None]
    normed = (stream_mid * inv_rms * norm_gain.astype(jnp.float32)).astype(jnp.bfloat16)
    keep_mask = valid_tok.astype(jnp.float32)[:, None]
    stream = (stream_mid * keep_mask).astype(jnp.bfloat16)
    normed_full = lax.all_gather(normed, ("blk", "rows"), axis=1, tiled=True)
    feature_width = gate_weight.shape[0]
    column_block = lax.dynamic_slice_in_dim(
        normed_full, lax.axis_index("heads") * feature_width, feature_width, 1
    )
    gate_part = jnp.dot(column_block, gate_weight, preferred_element_type=jnp.float32)
    up_part = jnp.dot(column_block, up_weight, preferred_element_type=jnp.float32)
    gate_rows, up_rows = (
        lax.psum(gate_part.astype(jnp.bfloat16), "heads").astype(jnp.float32),
        lax.psum(up_part.astype(jnp.bfloat16), "heads").astype(jnp.float32),
    )
    hidden = (jax.nn.gelu(gate_rows, approximate=True) * up_rows).astype(jnp.bfloat16)
    down_out = lax.psum_scatter(
        jnp.dot(hidden, down_weight, preferred_element_type=jnp.float32),
        ("blk", "rows"),
        scatter_dimension=0,
        tiled=True,
    )
    own_start = (lax.axis_index("blk") * lax.axis_size("rows") + lax.axis_index("rows")) * tok_dev
    keep_own = lax.dynamic_slice_in_dim(keep_mask, own_start, tok_dev, 0)
    return (stream, (down_out * keep_own).astype(jnp.bfloat16))


LANES = 128
MESH = pl.DeviceIdType.MESH
NEG = -1e30


def fits(sizes, queries, src_keys, dec_state, out_weight, gate_weight, down_weight):
    blocks, heads, rows = sizes
    tok_dev, local_heads, head_size = queries.shape
    width = out_weight.shape[1]
    return (
        heads == 2
        and rows == 2
        and blocks % heads == 0
        and local_heads == 8
        and tok_dev == 4
        and src_keys.shape[1] == 4
        and src_keys.shape[0] % LANES == 0
        and head_size == 2 * LANES
        and width % 64 == 0
        and gate_weight.shape[0] == width * blocks * rows // heads
        and gate_weight.shape[1] % (2 * LANES) == 0
        and down_weight.shape[1] % LANES == 0
        and dec_state.shape[0] <= 2 * LANES
        and gate_weight.size * 6 + src_keys.size * 8 <= 40 << 20
    )


def fused(
    sizes,
    q_ref,
    k_hbm,
    v_hbm,
    dec_ref,
    emb_ref,
    ow_hbm,
    gain_ref,
    gate_hbm,
    up_hbm,
    down_hbm,
    len_ref,
    pos_ref,
    stream_ref,
    branch_ref,
    kbuf,
    vbuf,
    sbuf,
    qall,
    att_send,
    att_recv,
    ag,
    agf,
    owbuf,
    pp_send,
    pp_recv,
    xb,
    sqb,
    gbuf,
    ubuf,
    dbuf,
    gu,
    gs_send,
    gs_recv,
    acc,
    dn_send,
    dn_recv,
    kv_sem,
    ow_sem,
    g_sem,
    u_sem,
    d_sem,
    q_ss,
    q_rs,
    a_ss,
    a_rs,
    ag_ss,
    ag_fs,
    ag_rs,
    p_ss,
    p_rs,
    x_ss,
    x_fs,
    x_rs,
    s_ss,
    s_rs,
    gs_ss,
    gs_rs,
    dn_ss,
    dn_rs,
):
    nb, nh, nr = sizes
    nj = nb * nr
    b = lax.axis_index("blk")
    h = lax.axis_index("heads")
    r = lax.axis_index("rows")
    me = b * nr + r
    other_row = 1 - r
    other_head = 1 - h
    own_rows = q_ref.shape[0]
    head_size = q_ref.shape[1]
    kv_heads = k_hbm.shape[1]
    src_len = k_hbm.shape[0]
    tokens, width = dec_ref.shape
    tok_dev = tokens // nj
    n_heads = own_rows // tok_dev
    n_chunks = gbuf.shape[0]
    chunk = gbuf.shape[2]
    f32 = jnp.float32
    bf16 = jnp.bfloat16

    for half in range(2):
        cols = pl.ds(half * LANES, LANES)
        pltpu.make_async_copy(k_hbm.at[:, :, cols], kbuf.at[half], kv_sem.at[half]).start()
    for half in range(2):
        cols = pl.ds(half * LANES, LANES)
        pltpu.make_async_copy(v_hbm.at[:, :, cols], vbuf.at[half], kv_sem.at[2 + half]).start()
    pltpu.make_async_copy(ow_hbm, owbuf, ow_sem).start()
    for c in range(n_chunks):
        cols = pl.ds(c * chunk, chunk)
        pltpu.make_async_copy(gate_hbm.at[:, cols], gbuf.at[c], g_sem.at[c]).start()
        pltpu.make_async_copy(up_hbm.at[:, cols], ubuf.at[c], u_sem.at[c]).start()
    for c in range(n_chunks):
        pltpu.make_async_copy(down_hbm.at[pl.ds(c * chunk, chunk)], dbuf.at[c], d_sem.at[c]).start()

    barrier = pltpu.get_barrier_semaphore()
    for d in range(1, nj):
        peer = lax.rem(me + d, nj)
        pl.semaphore_signal(
            barrier,
            inc=1,
            device_id={"blk": peer // nr, "rows": lax.rem(peer, nr)},
            device_id_type=MESH,
        )
    pl.semaphore_signal(barrier, inc=1, device_id={"heads": other_head}, device_id_type=MESH)
    pl.semaphore_wait(barrier, nj)

    def remote(source, target, send, recv, where):
        return pltpu.make_async_remote_copy(
            src_ref=source,
            dst_ref=target,
            send_sem=send,
            recv_sem=recv,
            device_id=where,
            device_id_type=MESH,
        )

    sent = []

    def send(*args):
        copy = remote(*args)
        copy.start()
        sent.append(copy)

    far = [lax.rem(b + d, nb) for d in range(1, nb)]
    partner = {"rows": other_row}

    for d, pb in enumerate(far):
        send(q_ref, qall.at[b], q_ss.at[d], q_rs.at[b], {"blk": pb})
    qall[b] = q_ref[...]
    for d, pb in enumerate(far):
        remote(q_ref, qall.at[pb], q_ss.at[d], q_rs.at[pb], {"blk": pb}).wait_recv()

    n_rows = nb * own_rows
    piece = LANES * kv_heads
    pieces = src_len // LANES
    query = qall[...].reshape(n_rows, head_size)
    row = lax.broadcasted_iota(jnp.int32, (n_rows, piece), 0)
    col = lax.broadcasted_iota(jnp.int32, (n_rows, piece), 1)
    fitting = (lax.rem(row, n_heads) // (n_heads // kv_heads)) == lax.rem(col, kv_heads)
    scale = head_size ** (-0.5)
    for half in range(2):
        cols = pl.ds(half * LANES, LANES)
        pltpu.make_async_copy(k_hbm.at[:, :, cols], kbuf.at[half], kv_sem.at[half]).wait()

    def load(buf, i):
        parts = [
            buf[half, pl.ds(i * LANES, LANES)].reshape(piece, LANES) for half in range(2)
        ]
        return jnp.concatenate(parts, axis=1)

    def score(i, top):
        found = lax.dot_general(
            query, load(kbuf, i), (((1,), (1,)), ((), ())), preferred_element_type=f32
        )
        found = jnp.where(fitting, found * scale, NEG)
        sbuf[i] = found
        for part in range(kv_heads):
            top = jnp.maximum(top, found[:, part * LANES : (part + 1) * LANES])
        return top

    top = lax.fori_loop(0, pieces, score, jnp.full((n_rows, LANES), NEG, f32))
    peak_bf = jnp.max(top, axis=1, keepdims=True).astype(bf16)
    left = lax.broadcasted_iota(jnp.int32, (n_rows, LANES), 1) < LANES // 2
    peak = peak_bf.astype(f32)
    for half in range(2):
        cols = pl.ds(half * LANES, LANES)
        pltpu.make_async_copy(v_hbm.at[:, :, cols], vbuf.at[half], kv_sem.at[2 + half]).wait()

    def weigh(i, carry):
        total, summed = carry
        weight = jnp.exp(sbuf[i] - peak)
        for part in range(kv_heads):
            total = total + weight[:, part * LANES : (part + 1) * LANES]
        summed = summed + jnp.dot(weight.astype(bf16), load(vbuf, i), preferred_element_type=f32)
        return total, summed

    total, summed = lax.fori_loop(
        0, pieces, weigh, (jnp.zeros((n_rows, LANES), f32), jnp.zeros((n_rows, head_size), f32))
    )
    total = jnp.sum(total, axis=1, keepdims=True)
    att_send[:, :, :head_size] = (summed / total).astype(bf16).reshape(nb, own_rows, head_size)
    stats = jnp.where(left, peak, total).astype(bf16)
    att_send[:, :, head_size:] = stats.reshape(nb, own_rows, LANES)

    for d, pb in enumerate(far):
        send(att_send.at[pb], att_recv.at[b], a_ss.at[d], a_rs.at[b], {"blk": pb})
    att_recv[b] = att_send[b]
    for d, pb in enumerate(far):
        remote(
            att_send.at[pb], att_recv.at[pb], a_ss.at[d], a_rs.at[pb], {"blk": pb}
        ).wait_recv()
    got = [att_recv[i].astype(f32) for i in range(nb)]
    peaks = [x[:, head_size : head_size + 1] for x in got]
    totals = [x[:, head_size + LANES // 2 : head_size + LANES // 2 + 1] for x in got]
    highest = peaks[0]
    for x in peaks[1:]:
        highest = jnp.maximum(highest, x)
    shares = [t * jnp.exp(p - highest) for t, p in zip(totals, peaks)]
    numer = shares[0] * got[0][:, :head_size]
    denom = shares[0]
    for x, share in zip(got[1:], shares[1:]):
        numer = numer + share * x[:, :head_size]
        denom = denom + share
    ag[me] = (numer / denom).astype(bf16)

    for d, pb in enumerate(far):
        send(ag.at[me], ag.at[me], ag_ss.at[d], ag_rs.at[me], {"blk": pb})
    send(ag.at[me], ag.at[me], ag_fs.at[b], ag_rs.at[me], partner)
    for d, pb in enumerate(far):
        j = pb * nr + r
        remote(ag.at[me], ag.at[j], ag_ss.at[d], ag_rs.at[j], {"blk": pb}).wait_recv()
        send(ag.at[j], ag.at[j], ag_fs.at[pb], ag_rs.at[j], partner)
    for pb in [b] + far:
        j = pb * nr + other_row
        remote(ag.at[j], ag.at[j], ag_fs.at[pb], ag_rs.at[j], partner).wait_recv()
    everyone = ag[...].astype(f32).reshape(nj * own_rows, head_size)
    for half in range(2):
        agf[half] = everyone[:, half * LANES : (half + 1) * LANES]
    pltpu.make_async_copy(ow_hbm, owbuf, ow_sem).wait()
    product = jnp.zeros((tokens, width), f32)
    for n in range(n_heads):
        parts = [agf[half, pl.ds(n, tokens, stride=n_heads), :] for half in range(2)]
        one = jnp.concatenate(parts, axis=1).astype(bf16)
        product = product + jnp.dot(
            one, owbuf[n * head_size : (n + 1) * head_size, :], preferred_element_type=f32
        )
    pp_send[...] = product.astype(bf16)
    send(pp_send, pp_recv, p_ss, p_rs, {"heads": other_head})

    def masks(start, count):
        token = lax.broadcasted_iota(jnp.int32, (count, 1), 0) + start
        place = lax.rem(token, LEN)
        which = token // LEN
        valid = jnp.zeros((count, 1), f32)
        hidden_slot = jnp.zeros((count, 1), f32)
        for c in range(pos_ref.shape[0]):
            here = (which == c).astype(f32)
            valid = valid + here * (place < len_ref[c]).astype(f32)
            same = (pos_ref[c : c + 1, :] == place).astype(f32)
            hidden_slot = hidden_slot + here * jnp.max(same, axis=1, keepdims=True)
        return valid, hidden_slot

    valid, hidden_slot = masks(0, tokens)
    base = jnp.where(hidden_slot > 0.5, emb_ref[...].astype(f32), dec_ref[...].astype(f32))
    gain = gain_ref[...].astype(f32)
    remote(pp_send, pp_recv, p_ss, p_rs, {"heads": other_head}).wait_recv()
    mid = base + (pp_send[...].astype(f32) + pp_recv[...].astype(f32))
    xb[me] = (mid * gain).astype(bf16)

    per = nb // nh
    mine = (b // per) == h

    @pl.when(mine)
    def _():
        for d, pb in enumerate(far):
            remote(xb.at[me], xb.at[me], x_ss.at[d], x_rs.at[me], {"blk": pb}).start()
        remote(xb.at[me], xb.at[me], x_fs.at[lax.rem(b, per)], x_rs.at[me], partner).start()

    sqb[me] = jnp.broadcast_to(jnp.sum(mid * mid, axis=1, keepdims=True), (tokens, LANES))
    stream_ref[...] = (mid * valid).astype(bf16)
    for d in range(1, nj):
        peer = lax.rem(me + d, nj)
        send(
            sqb.at[me],
            sqb.at[me],
            s_ss.at[d],
            s_rs.at[me],
            {"blk": peer // nr, "rows": lax.rem(peer, nr)},
        )
    for k in range(per):
        sb = h * per + k
        j = sb * nr + r

        @pl.when(sb != b)
        def _():
            remote(xb.at[j], xb.at[j], x_ss.at[0], x_rs.at[j], {"blk": sb}).wait_recv()
            remote(xb.at[j], xb.at[j], x_fs.at[k], x_rs.at[j], partner).start()

    for k in range(per):
        j = (h * per + k) * nr + other_row
        remote(xb.at[j], xb.at[j], x_fs.at[k], x_rs.at[j], partner).wait_recv()
    features = jnp.concatenate([xb[h * per * nr + k] for k in range(per * nr)], axis=1)

    def project(c, carry):
        cols = pl.ds(pl.multiple_of(c * chunk, chunk), chunk)
        pltpu.make_async_copy(gate_hbm.at[:, cols], gbuf.at[c], g_sem.at[c]).wait()
        gate = jnp.dot(features, gbuf[c], preferred_element_type=f32)
        gu[c, 0] = gate
        gs_send[c, 0] = gate.astype(bf16)
        pltpu.make_async_copy(up_hbm.at[:, cols], ubuf.at[c], u_sem.at[c]).wait()
        up = jnp.dot(features, ubuf[c], preferred_element_type=f32)
        gu[c, 1] = up
        gs_send[c, 1] = up.astype(bf16)
        remote(
            gs_send.at[c], gs_recv.at[c], gs_ss.at[c], gs_rs.at[c], {"heads": other_head}
        ).start()
        return carry

    lax.fori_loop(0, n_chunks, project, 0)

    squares = sqb[me]
    for d in range(1, nj):
        peer = lax.rem(me + d, nj)
        remote(
            sqb.at[peer],
            sqb.at[peer],
            s_ss.at[d],
            s_rs.at[peer],
            {"blk": peer // nr, "rows": lax.rem(peer, nr)},
        ).wait_recv()
        squares = squares + sqb[peer]
    inverse = lax.rsqrt(squares[:, :1] / (width * nj) + 1e-06)

    acc[...] = jnp.zeros_like(acc)

    def contract(c, carry):
        remote(
            gs_send.at[c], gs_recv.at[c], gs_ss.at[c], gs_rs.at[c], {"heads": other_head}
        ).wait()
        gate = (gu[c, 0] + gs_recv[c, 0].astype(f32)) * inverse
        up = (gu[c, 1] + gs_recv[c, 1].astype(f32)) * inverse
        hidden = (jax.nn.gelu(gate, approximate=True) * up).astype(bf16)
        pltpu.make_async_copy(
            down_hbm.at[pl.ds(pl.multiple_of(c * chunk, chunk), chunk)], dbuf.at[c], d_sem.at[c]
        ).wait()
        acc[...] += jnp.dot(hidden, dbuf[c], preferred_element_type=f32)
        return carry

    lax.fori_loop(0, n_chunks, contract, 0)

    for j in range(nj):
        dn_send[j] = acc[j * tok_dev : (j + 1) * tok_dev, :].astype(bf16)
    for d in range(1, nj):
        peer = lax.rem(me + d, nj)
        send(
            dn_send.at[peer],
            dn_recv.at[me],
            dn_ss.at[d],
            dn_rs.at[me],
            {"blk": peer // nr, "rows": lax.rem(peer, nr)},
        )
    result = dn_send[me].astype(f32)
    for d in range(1, nj):
        peer = lax.rem(me + d, nj)
        remote(
            dn_send.at[peer],
            dn_recv.at[peer],
            dn_ss.at[d],
            dn_rs.at[peer],
            {"blk": peer // nr, "rows": lax.rem(peer, nr)},
        ).wait_recv()
        result = result + dn_recv[peer].astype(f32)
    branch_ref[...] = (result * masks(me * tok_dev, tok_dev)[0]).astype(bf16)

    for copy in sent:
        copy.wait_send()

    @pl.when(mine)
    def _():
        for d, pb in enumerate(far):
            remote(xb.at[me], xb.at[me], x_ss.at[d], x_rs.at[me], {"blk": pb}).wait_send()

    for k in range(per):
        remote(xb.at[me], xb.at[me], x_fs.at[k], x_rs.at[me], partner).wait_send()


def kernel_call(sizes, *args):
    (
        queries,
        src_keys,
        src_values,
        dec_state,
        mask_embed,
        out_weight,
        norm_gain,
        gate_weight,
        up_weight,
        down_weight,
        cand_lengths,
        masked_pos,
    ) = args
    nb, nh, nr = sizes
    nj = nb * nr
    tok_dev, local_heads, head_size = queries.shape
    own_rows = tok_dev * local_heads
    src_len, kv_heads, _ = src_keys.shape
    tokens, width = dec_state.shape
    depth, hidden = gate_weight.shape
    out_width = down_weight.shape[1]
    chunk = 2 * LANES
    n_chunks = hidden // chunk
    f32 = jnp.float32
    bf16 = jnp.bfloat16
    dma = pltpu.SemaphoreType.DMA
    vmem = pl.BlockSpec(memory_space=pltpu.VMEM)
    anywhere = pl.BlockSpec(memory_space=pl.ANY)
    smem = pl.BlockSpec(memory_space=pltpu.SMEM)
    scratch = [
        pltpu.VMEM((2, src_len, kv_heads, LANES), bf16),
        pltpu.VMEM((2, src_len, kv_heads, LANES), bf16),
        pltpu.VMEM((src_len // LANES, nb * own_rows, kv_heads * LANES), f32),
        pltpu.VMEM((nb, own_rows, head_size), bf16),
        pltpu.VMEM((nb, own_rows, head_size + LANES), bf16),
        pltpu.VMEM((nb, own_rows, head_size + LANES), bf16),
        pltpu.VMEM((nj, own_rows, head_size), bf16),
        pltpu.VMEM((2, nj * own_rows, LANES), f32),
        pltpu.VMEM(out_weight.shape, bf16),
        pltpu.VMEM((tokens, width), bf16),
        pltpu.VMEM((tokens, width), bf16),
        pltpu.VMEM((nj, tokens, width), bf16),
        pltpu.VMEM((nj, tokens, LANES), f32),
        pltpu.VMEM((n_chunks, depth, chunk), bf16),
        pltpu.VMEM((n_chunks, depth, chunk), bf16),
        pltpu.VMEM((n_chunks, chunk, out_width), bf16),
        pltpu.VMEM((n_chunks, 2, tokens, chunk), f32),
        pltpu.VMEM((n_chunks, 2, tokens, chunk), bf16),
        pltpu.VMEM((n_chunks, 2, tokens, chunk), bf16),
        pltpu.VMEM((tokens, out_width), f32),
        pltpu.VMEM((nj, tok_dev, out_width), bf16),
        pltpu.VMEM((nj, tok_dev, out_width), bf16),
        dma((4,)),
        dma,
        dma((n_chunks,)),
        dma((n_chunks,)),
        dma((n_chunks,)),
        dma((nb,)),
        dma((nb,)),
        dma((nb,)),
        dma((nb,)),
        dma((nb,)),
        dma((nb,)),
        dma((nj,)),
        dma,
        dma,
        dma((nb,)),
        dma((nb,)),
        dma((nj,)),
        dma((nj,)),
        dma((nj,)),
        dma((n_chunks,)),
        dma((n_chunks,)),
        dma((nj,)),
        dma((nj,)),
    ]
    return tuple(
        pl.pallas_call(
            functools.partial(fused, sizes),
            out_shape=(
                jax.ShapeDtypeStruct((tokens, width), bf16),
                jax.ShapeDtypeStruct((tok_dev, out_width), bf16),
            ),
            in_specs=[
                vmem,
                anywhere,
                anywhere,
                vmem,
                vmem,
                anywhere,
                vmem,
                anywhere,
                anywhere,
                anywhere,
                smem,
                vmem,
            ],
            out_specs=(vmem, vmem),
            scratch_shapes=scratch,
            compiler_params=pltpu.CompilerParams(
                collective_id=0, has_side_effects=True, vmem_limit_bytes=56 << 20
            ),
        )(
            queries.reshape(own_rows, head_size),
            src_keys,
            src_values,
            dec_state,
            mask_embed.reshape(1, width),
            out_weight,
            norm_gain.reshape(1, width),
            gate_weight,
            up_weight,
            down_weight,
            cand_lengths,
            masked_pos,
        )
    )


def step(sizes, *args):
    queries, src_keys, _, dec_state, _, out_weight, _, gate_weight, _, down_weight, _, _ = args
    if fits(sizes, queries, src_keys, dec_state, out_weight, gate_weight, down_weight):
        return kernel_call(sizes, *args)
    return shards(*args)


def solution(mesh):
    sizes = tuple(mesh.shape[name] for name in ("blk", "heads", "rows"))
    placed = (
        P(("groups", "blk", "rows"), "heads", None),
        P(("groups", "blk"), "heads", None),
        P(("groups", "blk"), "heads", None),
        P("groups", ("blk", "rows")),
        P(("blk", "rows")),
        P("heads", ("blk", "rows")),
        P(("blk", "rows")),
        P("heads", ("blk", "rows")),
        P("heads", ("blk", "rows")),
        P(("blk", "rows"), "heads"),
        P("groups"),
        P("groups", None),
    )
    return jax.shard_map(
        functools.partial(step, sizes),
        mesh=mesh,
        in_specs=placed,
        out_specs=(P("groups", ("blk", "rows")), P(("groups", "blk", "rows"), "heads")),
        check_vma=False,
    )
```

```python
import functools

import jax
import jax.numpy as jnp
from jax import lax
from jax.experimental import pallas as pl
from jax.experimental.pallas import tpu as pltpu
from jax.sharding import PartitionSpec as P

D = 3584
LEN = 128


def token_masks(cand_lengths, masked_pos, tokens):
    positions = jnp.arange(tokens, dtype=jnp.int32) % LEN
    length_tok = jnp.repeat(cand_lengths, LEN)[:tokens]
    valid_tok = positions < length_tok
    slots = jnp.arange(LEN, dtype=jnp.int32)
    masked_tok = jnp.any(masked_pos[:, :, None] == slots[None, None, :], axis=1).reshape(-1)[
        :tokens
    ]
    return (valid_tok, masked_tok)


def shards(
    queries,
    src_keys,
    src_values,
    dec_state,
    mask_embed,
    out_weight,
    norm_gain,
    gate_weight,
    up_weight,
    down_weight,
    cand_lengths,
    masked_pos,
):
    tok_dev, local_heads, head_size = queries.shape
    kv_local = src_keys.shape[1]
    group_size = local_heads // kv_local
    score_scale = head_size ** (-0.5)
    queries_all = lax.all_gather(queries, "blk", axis=0, tiled=True)
    gathered_rows = queries_all.shape[0]
    grouped = queries_all.reshape(gathered_rows, kv_local, group_size, head_size)
    scores = (
        jnp.einsum("tgjd,kgd->tgjk", grouped, src_keys, preferred_element_type=jnp.float32)
        * score_scale
    )
    local_peak = jnp.max(scores, axis=3)
    weights = jnp.exp(scores - local_peak[..., None])
    totals = jnp.sum(weights, axis=3)
    numerator = jnp.einsum(
        "tgjk,kgd->tgjd",
        weights.astype(jnp.bfloat16),
        src_values,
        preferred_element_type=jnp.float32,
    )
    highest = lax.pmax(local_peak, "blk")
    factor = jnp.exp(local_peak - highest)
    numer_own, totals_own = (
        lax.psum_scatter(
            (numerator * factor[..., None]).astype(jnp.bfloat16),
            "blk",
            scatter_dimension=0,
            tiled=True,
        ).astype(jnp.float32),
        lax.psum_scatter(
            (totals * factor).astype(jnp.bfloat16), "blk", scatter_dimension=0, tiled=True
        ).astype(jnp.float32),
    )
    attn_own = (
        (numer_own / totals_own[..., None])
        .astype(jnp.bfloat16)
        .reshape(tok_dev, local_heads * head_size)
    )
    attn_all = lax.all_gather(attn_own, ("blk", "rows"), axis=0, tiled=True)
    tokens = attn_all.shape[0]
    projected = lax.psum(
        jnp.dot(attn_all, out_weight, preferred_element_type=jnp.float32).astype(jnp.bfloat16),
        "heads",
    ).astype(jnp.float32)
    valid_tok, masked_tok = token_masks(cand_lengths, masked_pos, tokens)
    base_state = jnp.where(masked_tok[:, None], mask_embed[None, :], dec_state).astype(jnp.float32)
    stream_mid = base_state + projected
    squares = lax.psum(jnp.sum(stream_mid * stream_mid, axis=1), ("blk", "rows"))
    inv_rms = lax.rsqrt(squares / D + 1e-06)[:, None]
    normed = (stream_mid * inv_rms * norm_gain.astype(jnp.float32)).astype(jnp.bfloat16)
    keep_mask = valid_tok.astype(jnp.float32)[:, None]
    stream = (stream_mid * keep_mask).astype(jnp.bfloat16)
    normed_full = lax.all_gather(normed, ("blk", "rows"), axis=1, tiled=True)
    feature_width = gate_weight.shape[0]
    column_block = lax.dynamic_slice_in_dim(
        normed_full, lax.axis_index("heads") * feature_width, feature_width, 1
    )
    gate_part = jnp.dot(column_block, gate_weight, preferred_element_type=jnp.float32)
    up_part = jnp.dot(column_block, up_weight, preferred_element_type=jnp.float32)
    gate_rows, up_rows = (
        lax.psum(gate_part.astype(jnp.bfloat16), "heads").astype(jnp.float32),
        lax.psum(up_part.astype(jnp.bfloat16), "heads").astype(jnp.float32),
    )
    hidden = (jax.nn.gelu(gate_rows, approximate=True) * up_rows).astype(jnp.bfloat16)
    down_out = lax.psum_scatter(
        jnp.dot(hidden, down_weight, preferred_element_type=jnp.float32),
        ("blk", "rows"),
        scatter_dimension=0,
        tiled=True,
    )
    own_start = (lax.axis_index("blk") * lax.axis_size("rows") + lax.axis_index("rows")) * tok_dev
    keep_own = lax.dynamic_slice_in_dim(keep_mask, own_start, tok_dev, 0)
    return (stream, (down_out * keep_own).astype(jnp.bfloat16))


LANES = 128
MESH = pl.DeviceIdType.MESH
NEG = -1e30


def fits(sizes, queries, src_keys, dec_state, out_weight, gate_weight, down_weight):
    blocks, heads, rows = sizes
    tok_dev, local_heads, head_size = queries.shape
    width = out_weight.shape[1]
    return (
        heads == 2
        and rows == 2
        and blocks % heads == 0
        and local_heads == 8
        and tok_dev == 4
        and src_keys.shape[1] == 4
        and src_keys.shape[0] % LANES == 0
        and head_size == 2 * LANES
        and width % 64 == 0
        and gate_weight.shape[0] == width * blocks * rows // heads
        and gate_weight.shape[1] % (2 * LANES) == 0
        and down_weight.shape[1] % (2 * LANES) == 0
        and dec_state.shape[0] <= 2 * LANES
        and gate_weight.size * 6 + src_keys.size * 8 <= 40 << 20
    )


def fused(
    sizes,
    q_ref,
    k_hbm,
    v_hbm,
    dec_hbm,
    emb_hbm,
    ow_hbm,
    gain_hbm,
    gate_hbm,
    up_hbm,
    down_hbm,
    len_hbm,
    pos_hbm,
    stream_ref,
    branch_ref,
    kbuf,
    vbuf,
    sbuf,
    qall,
    att_send,
    att_recv,
    ag,
    agf,
    owbuf,
    pp_send,
    pp_recv,
    xb,
    sqb,
    gbuf,
    ubuf,
    dbuf,
    gu,
    gs_send,
    gs_recv,
    units,
    acc,
    dn_send,
    dn_recv,
    dec_ref,
    emb_ref,
    gain_ref,
    len_ref,
    pos_ref,
    small_sem,
    kv_sem,
    ow_sem,
    g_sem,
    u_sem,
    d_sem,
    q_ss,
    q_rs,
    a_ss,
    a_rs,
    ag_ss,
    ag_fs,
    ag_rs,
    p_ss,
    p_rs,
    x_ss,
    x_fs,
    x_rs,
    s_ss,
    s_rs,
    gs_ss,
    gs_rs,
    dn_ss,
    dn_rs,
):
    nb, nh, nr = sizes
    nj = nb * nr
    b = lax.axis_index("blk")
    h = lax.axis_index("heads")
    r = lax.axis_index("rows")
    me = b * nr + r
    other_row = 1 - r
    other_head = 1 - h
    own_rows = q_ref.shape[0]
    head_size = q_ref.shape[1]
    kv_heads = k_hbm.shape[1]
    src_len = k_hbm.shape[0]
    tokens, width = dec_hbm.shape
    tok_dev = tokens // nj
    n_heads = own_rows // tok_dev
    n_chunks = gbuf.shape[0]
    chunk = gbuf.shape[2]
    f32 = jnp.float32
    bf16 = jnp.bfloat16

    small = [
        pltpu.make_async_copy(source, target, small_sem.at[i])
        for i, (source, target) in enumerate(
            [
                (q_ref, qall.at[b]),
                (dec_hbm, dec_ref),
                (emb_hbm, emb_ref),
                (gain_hbm, gain_ref),
                (len_hbm, len_ref),
                (pos_hbm, pos_ref),
            ]
        )
    ]
    for copy in small:
        copy.start()
    for half in range(2):
        cols = pl.ds(half * LANES, LANES)
        pltpu.make_async_copy(k_hbm.at[:, :, cols], kbuf.at[half], kv_sem.at[half]).start()
    for half in range(2):
        cols = pl.ds(half * LANES, LANES)
        pltpu.make_async_copy(v_hbm.at[:, :, cols], vbuf.at[half], kv_sem.at[2 + half]).start()
    barrier = pltpu.get_barrier_semaphore()
    for d in range(1, nj):
        peer = lax.rem(me + d, nj)
        pl.semaphore_signal(
            barrier,
            inc=1,
            device_id={"blk": peer // nr, "rows": lax.rem(peer, nr)},
            device_id_type=MESH,
        )
    pl.semaphore_signal(barrier, inc=1, device_id={"heads": other_head}, device_id_type=MESH)
    pl.semaphore_wait(barrier, nj)

    def remote(source, target, send, recv, where):
        return pltpu.make_async_remote_copy(
            src_ref=source,
            dst_ref=target,
            send_sem=send,
            recv_sem=recv,
            device_id=where,
            device_id_type=MESH,
        )

    sent = []

    def send(*args):
        copy = remote(*args)
        copy.start()
        sent.append(copy)

    far = [lax.rem(b + d, nb) for d in range(1, nb)]
    partner = {"rows": other_row}

    for d, pb in enumerate(far):
        send(q_ref, qall.at[b], q_ss.at[d], q_rs.at[b], {"blk": pb})
    small[0].wait()

    for copy in small[1:]:
        copy.wait()

    def masks(start, count):
        token = lax.broadcasted_iota(jnp.int32, (count, 1), 0) + start
        place = lax.rem(token, LEN)
        which = token // LEN
        valid = jnp.zeros((count, 1), f32)
        hidden_slot = jnp.zeros((count, 1), f32)
        for c in range(pos_ref.shape[0]):
            here = (which == c).astype(f32)
            valid = valid + here * (place < len_ref[c]).astype(f32)
            same = (pos_ref[c : c + 1, :] == place).astype(f32)
            hidden_slot = hidden_slot + here * jnp.max(same, axis=1, keepdims=True)
        return valid, hidden_slot

    valid, hidden_slot = masks(0, tokens)
    own_valid = masks(me * tok_dev, tok_dev)[0]
    base = jnp.where(hidden_slot > 0.5, emb_ref[...].astype(f32)[None, :], dec_ref[...].astype(f32))
    gain = gain_ref[...].astype(f32)[None, :]
    for d, pb in enumerate(far):
        remote(q_ref, qall.at[pb], q_ss.at[d], q_rs.at[pb], {"blk": pb}).wait_recv()

    n_rows = nb * own_rows
    piece = LANES * kv_heads
    pieces = src_len // LANES
    unroll = 4 if pieces % 4 == 0 else 1
    query = qall[...].reshape(n_rows, head_size)
    row = lax.broadcasted_iota(jnp.int32, (n_rows, piece), 0)
    col = lax.broadcasted_iota(jnp.int32, (n_rows, piece), 1)
    fitting = (lax.rem(row, n_heads) // (n_heads // kv_heads)) == lax.rem(col, kv_heads)
    scale = head_size ** (-0.5)
    for half in range(2):
        cols = pl.ds(half * LANES, LANES)
        pltpu.make_async_copy(k_hbm.at[:, :, cols], kbuf.at[half], kv_sem.at[half]).wait()

    def load(buf, i):
        parts = [
            buf[half, pl.ds(i * LANES, LANES)].reshape(piece, LANES) for half in range(2)
        ]
        return jnp.concatenate(parts, axis=1)

    def score(i, top):
        found = lax.dot_general(
            query, load(kbuf, i), (((1,), (1,)), ((), ())), preferred_element_type=f32
        )
        found = jnp.where(fitting, found * scale, NEG)
        sbuf[i] = found
        for part in range(kv_heads):
            top = jnp.maximum(top, found[:, part * LANES : (part + 1) * LANES])
        return top

    def several(one):
        def run(i, carry):
            for u in range(unroll):
                carry = one(i * unroll + u, carry)
            return carry

        return run

    top = lax.fori_loop(
        0, pieces // unroll, several(score), jnp.full((n_rows, LANES), NEG, f32)
    )
    peak_bf = jnp.max(top, axis=1, keepdims=True).astype(bf16)
    left = lax.broadcasted_iota(jnp.int32, (n_rows, LANES), 1) < LANES // 2
    peak = peak_bf.astype(f32)
    for half in range(2):
        cols = pl.ds(half * LANES, LANES)
        pltpu.make_async_copy(v_hbm.at[:, :, cols], vbuf.at[half], kv_sem.at[2 + half]).wait()
    pltpu.make_async_copy(ow_hbm, owbuf, ow_sem).start()
    for c in range(n_chunks):
        cols = pl.ds(c * chunk, chunk)
        pltpu.make_async_copy(gate_hbm.at[:, cols], gbuf.at[c], g_sem.at[c]).start()
        pltpu.make_async_copy(up_hbm.at[:, cols], ubuf.at[c], u_sem.at[c]).start()
    for c in range(n_chunks):
        pltpu.make_async_copy(down_hbm.at[pl.ds(c * chunk, chunk)], dbuf.at[c], d_sem.at[c]).start()

    def weigh(i, carry):
        total, summed = carry
        weight = jnp.exp(sbuf[i] - peak)
        for part in range(kv_heads):
            total = total + weight[:, part * LANES : (part + 1) * LANES]
        summed = summed + jnp.dot(weight.astype(bf16), load(vbuf, i), preferred_element_type=f32)
        return total, summed

    total, summed = lax.fori_loop(
        0,
        pieces // unroll,
        several(weigh),
        (jnp.zeros((n_rows, LANES), f32), jnp.zeros((n_rows, head_size), f32)),
    )
    total = jnp.sum(total, axis=1, keepdims=True)
    att_send[:, :, :head_size] = (summed / total).astype(bf16).reshape(nb, own_rows, head_size)
    stats = jnp.where(left, peak, total).astype(bf16)
    att_send[:, :, head_size:] = stats.reshape(nb, own_rows, LANES)

    for d, pb in enumerate(far):
        send(att_send.at[pb], att_recv.at[b], a_ss.at[d], a_rs.at[b], {"blk": pb})
    att_recv[b] = att_send[b]
    for d, pb in enumerate(far):
        remote(
            att_send.at[pb], att_recv.at[pb], a_ss.at[d], a_rs.at[pb], {"blk": pb}
        ).wait_recv()
    got = [att_recv[i].astype(f32) for i in range(nb)]
    peaks = [x[:, head_size : head_size + 1] for x in got]
    totals = [x[:, head_size + LANES // 2 : head_size + LANES // 2 + 1] for x in got]
    highest = peaks[0]
    for x in peaks[1:]:
        highest = jnp.maximum(highest, x)
    shares = [t * jnp.exp(p - highest) for t, p in zip(totals, peaks)]
    numer = shares[0] * got[0][:, :head_size]
    denom = shares[0]
    for x, share in zip(got[1:], shares[1:]):
        numer = numer + share * x[:, :head_size]
        denom = denom + share
    ag[me] = (numer / denom).astype(bf16)

    for d, pb in enumerate(far):
        send(ag.at[me], ag.at[me], ag_ss.at[d], ag_rs.at[me], {"blk": pb})
    send(ag.at[me], ag.at[me], ag_fs.at[b], ag_rs.at[me], partner)
    for d, pb in enumerate(far):
        j = pb * nr + r
        remote(ag.at[me], ag.at[j], ag_ss.at[d], ag_rs.at[j], {"blk": pb}).wait_recv()
        send(ag.at[j], ag.at[j], ag_fs.at[pb], ag_rs.at[j], partner)
    for pb in [b] + far:
        j = pb * nr + other_row
        remote(ag.at[j], ag.at[j], ag_fs.at[pb], ag_rs.at[j], partner).wait_recv()
    everyone = ag[...].astype(f32).reshape(nj * own_rows, head_size)
    for half in range(2):
        agf[half] = everyone[:, half * LANES : (half + 1) * LANES]
    pltpu.make_async_copy(ow_hbm, owbuf, ow_sem).wait()
    product = jnp.zeros((tokens, width), f32)
    for n in range(n_heads):
        parts = [agf[half, pl.ds(n, tokens, stride=n_heads), :] for half in range(2)]
        one = jnp.concatenate(parts, axis=1).astype(bf16)
        product = product + lax.dot_general(
            one,
            owbuf[:, n * head_size : (n + 1) * head_size],
            (((1,), (1,)), ((), ())),
            preferred_element_type=f32,
        )
    pp_send[...] = product.astype(bf16)
    send(pp_send, pp_recv, p_ss, p_rs, {"heads": other_head})

    remote(pp_send, pp_recv, p_ss, p_rs, {"heads": other_head}).wait_recv()
    mid = base + (pp_send[...].astype(f32) + pp_recv[...].astype(f32))
    xb[me] = (mid * gain).astype(bf16)

    per = nb // nh
    mine = (b // per) == h

    @pl.when(mine)
    def _():
        for d, pb in enumerate(far):
            remote(xb.at[me], xb.at[me], x_ss.at[d], x_rs.at[me], {"blk": pb}).start()
        remote(xb.at[me], xb.at[me], x_fs.at[lax.rem(b, per)], x_rs.at[me], partner).start()

    sqb[me] = jnp.broadcast_to(jnp.sum(mid * mid, axis=1, keepdims=True), (tokens, LANES))
    stream_ref[...] = (mid * valid).astype(bf16)
    for d in range(1, nj):
        peer = lax.rem(me + d, nj)
        send(
            sqb.at[me],
            sqb.at[me],
            s_ss.at[d],
            s_rs.at[me],
            {"blk": peer // nr, "rows": lax.rem(peer, nr)},
        )
    for k in range(per):
        sb = h * per + k
        j = sb * nr + r

        @pl.when(sb != b)
        def _():
            remote(xb.at[j], xb.at[j], x_ss.at[0], x_rs.at[j], {"blk": sb}).wait_recv()
            remote(xb.at[j], xb.at[j], x_fs.at[k], x_rs.at[j], partner).start()

    for k in range(per):
        j = (h * per + k) * nr + other_row
        remote(xb.at[j], xb.at[j], x_fs.at[k], x_rs.at[j], partner).wait_recv()
    features = jnp.concatenate([xb[h * per * nr + k] for k in range(per * nr)], axis=1)

    def project(c, carry):
        cols = pl.ds(pl.multiple_of(c * chunk, chunk), chunk)
        pltpu.make_async_copy(gate_hbm.at[:, cols], gbuf.at[c], g_sem.at[c]).wait()
        gate = jnp.dot(features, gbuf[c], preferred_element_type=f32)
        gu[c, 0] = gate
        gs_send[c, 0] = gate.astype(bf16)
        pltpu.make_async_copy(up_hbm.at[:, cols], ubuf.at[c], u_sem.at[c]).wait()
        up = jnp.dot(features, ubuf[c], preferred_element_type=f32)
        gu[c, 1] = up
        gs_send[c, 1] = up.astype(bf16)
        remote(
            gs_send.at[c], gs_recv.at[c], gs_ss.at[c], gs_rs.at[c], {"heads": other_head}
        ).start()
        return carry

    lax.fori_loop(0, n_chunks, project, 0)

    squares = sqb[me]
    for d in range(1, nj):
        peer = lax.rem(me + d, nj)
        remote(
            sqb.at[peer],
            sqb.at[peer],
            s_ss.at[d],
            s_rs.at[peer],
            {"blk": peer // nr, "rows": lax.rem(peer, nr)},
        ).wait_recv()
        squares = squares + sqb[peer]
    inverse = lax.rsqrt(squares[:, :1] / (width * nj) + 1e-06)

    span = acc.shape[2]
    acc[...] = jnp.zeros_like(acc)

    def contract(c, carry):
        remote(
            gs_send.at[c], gs_recv.at[c], gs_ss.at[c], gs_rs.at[c], {"heads": other_head}
        ).wait()
        gate = (gu[c, 0] + gs_recv[c, 0].astype(f32)) * inverse
        up = (gu[c, 1] + gs_recv[c, 1].astype(f32)) * inverse
        hidden = (jax.nn.gelu(gate, approximate=True) * up).astype(bf16)
        units[c] = hidden
        pltpu.make_async_copy(
            down_hbm.at[pl.ds(pl.multiple_of(c * chunk, chunk), chunk)], dbuf.at[c], d_sem.at[c]
        ).wait()
        acc[0] += jnp.dot(hidden, dbuf[c, :, :span], preferred_element_type=f32)
        return carry

    lax.fori_loop(0, n_chunks, contract, 0)

    def peer_of(d):
        peer = lax.rem(me + d, nj)
        return peer, {"blk": peer // nr, "rows": lax.rem(peer, nr)}

    def hand_out(part):
        for j in range(nj):
            dn_send[part, j] = acc[part, j * tok_dev : (j + 1) * tok_dev, :].astype(bf16)
        for d in range(1, nj):
            peer, where = peer_of(d)
            send(
                dn_send.at[part, peer],
                dn_recv.at[part, me],
                dn_ss.at[part, d],
                dn_rs.at[part, me],
                where,
            )

    hand_out(0)

    def contract_rest(c, carry):
        acc[1] += jnp.dot(units[c], dbuf[c, :, span:], preferred_element_type=f32)
        return carry

    lax.fori_loop(0, n_chunks, contract_rest, 0)
    hand_out(1)
    for part in range(2):
        result = dn_send[part, me].astype(f32)
        for d in range(1, nj):
            peer, where = peer_of(d)
            remote(
                dn_send.at[part, peer],
                dn_recv.at[part, peer],
                dn_ss.at[part, d],
                dn_rs.at[part, peer],
                where,
            ).wait_recv()
            result = result + dn_recv[part, peer].astype(f32)
        branch_ref[:, part * span : (part + 1) * span] = (result * own_valid).astype(bf16)

    for copy in sent:
        copy.wait_send()

    @pl.when(mine)
    def _():
        for d, pb in enumerate(far):
            remote(xb.at[me], xb.at[me], x_ss.at[d], x_rs.at[me], {"blk": pb}).wait_send()

    for k in range(per):
        remote(xb.at[me], xb.at[me], x_fs.at[k], x_rs.at[me], partner).wait_send()


def kernel_call(sizes, *args):
    (
        queries,
        src_keys,
        src_values,
        dec_state,
        mask_embed,
        out_weight,
        norm_gain,
        gate_weight,
        up_weight,
        down_weight,
        cand_lengths,
        masked_pos,
    ) = args
    nb, nh, nr = sizes
    nj = nb * nr
    tok_dev, local_heads, head_size = queries.shape
    own_rows = tok_dev * local_heads
    src_len, kv_heads, _ = src_keys.shape
    tokens, width = dec_state.shape
    depth, hidden = gate_weight.shape
    out_width = down_weight.shape[1]
    chunk = 2 * LANES
    n_chunks = hidden // chunk
    f32 = jnp.float32
    bf16 = jnp.bfloat16
    dma = pltpu.SemaphoreType.DMA
    vmem = pl.BlockSpec(memory_space=pltpu.VMEM)
    anywhere = pl.BlockSpec(memory_space=pl.ANY)
    scratch = [
        pltpu.VMEM((2, src_len, kv_heads, LANES), bf16),
        pltpu.VMEM((2, src_len, kv_heads, LANES), bf16),
        pltpu.VMEM((src_len // LANES, nb * own_rows, kv_heads * LANES), f32),
        pltpu.VMEM((nb, own_rows, head_size), bf16),
        pltpu.VMEM((nb, own_rows, head_size + LANES), bf16),
        pltpu.VMEM((nb, own_rows, head_size + LANES), bf16),
        pltpu.VMEM((nj, own_rows, head_size), bf16),
        pltpu.VMEM((2, nj * own_rows, LANES), f32),
        pltpu.VMEM(out_weight.shape[::-1], bf16),
        pltpu.VMEM((tokens, width), bf16),
        pltpu.VMEM((tokens, width), bf16),
        pltpu.VMEM((nj, tokens, width), bf16),
        pltpu.VMEM((nj, tokens, LANES), f32),
        pltpu.VMEM((n_chunks, depth, chunk), bf16),
        pltpu.VMEM((n_chunks, depth, chunk), bf16),
        pltpu.VMEM((n_chunks, chunk, out_width), bf16),
        pltpu.VMEM((n_chunks, 2, tokens, chunk), f32),
        pltpu.VMEM((n_chunks, 2, tokens, chunk), bf16),
        pltpu.VMEM((n_chunks, 2, tokens, chunk), bf16),
        pltpu.VMEM((n_chunks, tokens, chunk), bf16),
        pltpu.VMEM((2, tokens, out_width // 2), f32),
        pltpu.VMEM((2, nj, tok_dev, out_width // 2), bf16),
        pltpu.VMEM((2, nj, tok_dev, out_width // 2), bf16),
        pltpu.VMEM(dec_state.shape, bf16),
        pltpu.VMEM(mask_embed.shape, bf16),
        pltpu.VMEM(norm_gain.shape, bf16),
        pltpu.SMEM(cand_lengths.shape, jnp.int32),
        pltpu.VMEM(masked_pos.shape, jnp.int32),
        dma((6,)),
        dma((4,)),
        dma,
        dma((n_chunks,)),
        dma((n_chunks,)),
        dma((n_chunks,)),
        dma((nb,)),
        dma((nb,)),
        dma((nb,)),
        dma((nb,)),
        dma((nb,)),
        dma((nb,)),
        dma((nj,)),
        dma,
        dma,
        dma((nb,)),
        dma((nb,)),
        dma((nj,)),
        dma((nj,)),
        dma((nj,)),
        dma((n_chunks,)),
        dma((n_chunks,)),
        dma((2, nj)),
        dma((2, nj)),
    ]
    results = tuple(
        pl.pallas_call(
            functools.partial(fused, sizes),
            out_shape=(
                jax.ShapeDtypeStruct((tokens, width), bf16),
                jax.ShapeDtypeStruct((tok_dev, out_width), bf16),
            ),
            in_specs=[anywhere] * 12,
            out_specs=(vmem, vmem),
            scratch_shapes=scratch,
            compiler_params=pltpu.CompilerParams(
                collective_id=0, has_side_effects=True, vmem_limit_bytes=56 << 20
            ),
        )(
            queries.reshape(own_rows, head_size),
            src_keys,
            src_values,
            dec_state,
            mask_embed,
            out_weight.T,
            norm_gain,
            gate_weight,
            up_weight,
            down_weight,
            cand_lengths,
            masked_pos,
        )
    )
    return tuple(
        pl.pallas_call(
            hand_on,
            out_shape=tuple(jax.ShapeDtypeStruct(x.shape, x.dtype) for x in results),
            in_specs=[vmem, vmem],
            out_specs=(vmem, vmem),
        )(*results)
    )


def hand_on(stream_in, branch_in, stream_out, branch_out):
    stream_out[...] = stream_in[...]
    branch_out[...] = branch_in[...]


def step(sizes, *args):
    queries, src_keys, _, dec_state, _, out_weight, _, gate_weight, _, down_weight, _, _ = args
    if fits(sizes, queries, src_keys, dec_state, out_weight, gate_weight, down_weight):
        return kernel_call(sizes, *args)
    return shards(*args)


def solution(mesh):
    sizes = tuple(mesh.shape[name] for name in ("blk", "heads", "rows"))
    placed = (
        P(("groups", "blk", "rows"), "heads", None),
        P(("groups", "blk"), "heads", None),
        P(("groups", "blk"), "heads", None),
        P("groups", ("blk", "rows")),
        P(("blk", "rows")),
        P("heads", ("blk", "rows")),
        P(("blk", "rows")),
        P("heads", ("blk", "rows")),
        P("heads", ("blk", "rows")),
        P(("blk", "rows"), "heads"),
        P("groups"),
        P("groups", None),
    )
    return jax.shard_map(
        functools.partial(step, sizes),
        mesh=mesh,
        in_specs=placed,
        out_specs=(P("groups", ("blk", "rows")), P(("groups", "blk", "rows"), "heads")),
        check_vma=False,
    )
```
